128 devices in a mesh: gx: 4 (over z_lo, core), gy: 4 (over y), gz: 8 (over z_hi, x).
Axes of the slice: x: 4, y: 4, z: 4 (z_hi: 2, z_lo: 2; z = z_hi * 2 + z_lo), core: 2. Of those that a mesh axis runs over, the one named last changes fastest.
Arguments:
- e_field: float32 [3, 24, 1024, 2048], P(None, None, ('gx', 'gy'), 'gz'), may hold values from -6 to 6
- h_field: float32 [3, 24, 1024, 2048], P(None, None, ('gx', 'gy'), 'gz'), may hold values from -6 to 6
- material: int32 [24, 1024, 2048], P(None, ('gx', 'gy'), 'gz'), may hold values from 0 to 15
- decay_table: float32 [2, 16], replicated, may hold values from 0.6 to 1
- curl_table: float32 [2, 16], replicated, may hold values from 0.25 to 0.55
- residues: float32 [8, 16, 1024, 1024], P('gz', 'gy', 'gx'), may hold values from -0.046875 to 0.046875
- pole_decay: float32 [8, 16], P('gz', 'gy'), may hold values from 0.05 to 0.98
- pole_states: float32 [8, 16, 1024], P('gz', 'gy'), may hold values from -6 to 6
- direct: float32 [8, 1024], P('gz', 'gx'), may hold values from 0.2 to 1
- port_cell: int32 [8192], P(('gx', 'gy', 'gz')), may hold values from 0 to 393215
- port_owner: int32 [8192], P(('gx', 'gy', 'gz')), may hold values from 0 to 8191, each once
Outputs:
- e_out: float32 [3, 24, 1024, 2048], P(None, None, ('gx', 'gy'), 'gz')
- h_out: float32 [3, 24, 1024, 2048], P(None, None, ('gx', 'gy'), 'gz')
- states_out: float32 [8, 16, 1024], P('gz', 'gy')
The draws below stay inside these ranges and needn't reach their ends.
Inputs may be any that keep to these rules, and one draw needn't show every extreme that they name: material ids index the tables. `port_cell`: a cell of the block of the device that holds the slot, numbered (i * 64 + j) * 256 + k; several slots may share a cell. `port_owner`: every port appears in exactly one slot.
All inputs are finite; a program needn't handle non-finite values.
Results may differ from the reference program's by a relative error of at most 0.0001.
Values sent between devices are 32-bit elements; how exact they have to be, the bound alone decides.
No kernel may reach another device: no remote copies, remote signals or barrier semaphores. Data moves between devices by JAX's collectives and lax.ppermute only.
A program may use at most 128 MiB of HBM per device.

```python
import math
import jax
import jax.numpy as jnp
from jax import lax

CX = 24
CY = 64
CZ = 256
DP = 1024
NPOLE = 16
NMAT = 16
STEPS = 2
NX = 24
NY = 1024
NZ = 2048
NDIE = 8
P_SIZE = 8192
SLOT_DEV = 64
N_GY = 4
N_GZ = 8


def place_ends(result, stream_key, smallest, largest):
    extent = result.shape
    index_at = [jax.random.randint(jax.random.fold_in(stream_key, axis), (), 0, extent[axis]) for axis in range(len(extent))]
    result = result.at[tuple(index_at)].set(smallest)
    longest = extent.index(max(extent))
    index_at[longest] = (index_at[longest] + 1) % extent[longest]
    return result.at[tuple(index_at)].set(largest)


def levels(key, extent, cuts, low, high):
    def one(axis_at, blocks):
        heights = jax.random.uniform(jax.random.fold_in(jax.random.fold_in(key, 6), axis_at), (blocks,), jnp.float32, low / len(cuts), high / len(cuts))
        return jnp.repeat(jnp.exp(heights), extent[axis_at] // blocks).reshape((-1,) + (1,) * (len(extent) - axis_at - 1))

    gain = one(*cuts[0])
    for cut in cuts[1:]:
        gain = gain * one(*cut)
    return gain


def scatter_about(key, dims, width, reach, split=(), kind=jnp.bfloat16):
    values = jax.random.normal(key, dims, jnp.float32) * width
    if len(split) > 0:
        values = levels(key, dims, split, -0.22, 0.18) * values
    return jnp.clip(values, min=-reach, max=reach).astype(kind)


def setup_inputs(seed: int = 0) -> dict:
    streams_of = jax.random.split(jax.random.key(seed), 12)
    return {
        "e_field": scatter_about(streams_of[0], (3, NX, NY, NZ), 1.0, 6.0, ((2, 16), (3, 8)), jnp.float32),
        "h_field": scatter_about(streams_of[1], (3, NX, NY, NZ), 1.0, 6.0, ((2, 16), (3, 8)), jnp.float32),
        "material": place_ends(jax.random.randint(streams_of[2], (NX, NY, NZ), 0, NMAT), jax.random.fold_in(streams_of[2], 1), 0, NMAT - 1).astype(jnp.int32),
        "decay_table": jnp.clip(jax.random.uniform(streams_of[3], (2, NMAT), jnp.float32, 0.6, 1.0), 0.6, 1.0),
        "curl_table": jnp.clip(jax.random.uniform(streams_of[4], (2, NMAT), jnp.float32, 0.25, 0.55), 0.25, 0.55),
        "residues": scatter_about(streams_of[5], (NDIE, NPOLE, DP, DP), (NPOLE * DP) ** -0.5, 0.046875, ((0, 8), (1, 4), (2, 4)), jnp.float32),
        "pole_decay": jnp.clip(jnp.exp(math.log(0.98) - 2.9755296 * jax.random.uniform(streams_of[6], (NDIE, NPOLE), jnp.float32) ** levels(streams_of[6], (NDIE, NPOLE), ((0, 8), (1, 4)), -0.2, 0.2)), 0.05, 0.98),
        "pole_states": scatter_about(streams_of[7], (NDIE, NPOLE, DP), 1.0, 6.0, ((0, 8), (1, 4)), jnp.float32),
        "direct": jnp.clip(0.2 + 0.8 * jax.random.uniform(streams_of[8], (NDIE, DP), jnp.float32) ** levels(streams_of[8], (NDIE, DP), ((0, 8), (1, 4)), -0.2, 0.2), 0.2, 1.0),
        "port_cell": place_ends(jax.random.randint(streams_of[9], (P_SIZE,), 0, CX * CY * CZ), jax.random.fold_in(streams_of[9], 1), 0, (CX * CY * CZ) - 1).astype(jnp.int32),
        "port_owner": jax.random.permutation(streams_of[10], P_SIZE).astype(jnp.int32),
    }


def forward(field, axis):
    inner = lax.slice_in_dim(field, 1, field.shape[axis], axis=axis)
    border = jnp.zeros_like(lax.slice_in_dim(field, 0, 1, axis=axis))
    return jnp.concatenate([inner, border], axis)


def backward(field, axis):
    inner = lax.slice_in_dim(field, 0, field.shape[axis] - 1, axis=axis)
    border = jnp.zeros_like(lax.slice_in_dim(field, 0, 1, axis=axis))
    return jnp.concatenate([border, inner], axis)


def magnetic_update(electric, magnetic, ahead, decay, curl):
    first = decay * magnetic[0] - curl * ((ahead[0] - electric[2]) - (ahead[1] - electric[1]))
    second = decay * magnetic[1] - curl * ((ahead[2] - electric[0]) - (ahead[3] - electric[2]))
    third = decay * magnetic[2] - curl * ((ahead[4] - electric[1]) - (ahead[5] - electric[0]))
    return (first, second, third)


def electric_update(electric, magnetic, behind, decay, curl, source):
    first = decay * electric[0] + curl * ((magnetic[2] - behind[0]) - (magnetic[1] - behind[1]))
    second = decay * electric[1] + curl * ((magnetic[0] - behind[2]) - (magnetic[2] - behind[3]))
    third = decay * electric[2] + curl * (((magnetic[1] - behind[4]) - (magnetic[0] - behind[5])) - source)
    return (first, second, third)


def reference(e_field, h_field, material, decay_table, curl_table, residues, pole_decay, pole_states, direct, port_cell, port_owner):
    decay_elec = decay_table[0][material]
    decay_magn = decay_table[1][material]
    curl_elec = curl_table[0][material]
    curl_magn = curl_table[1][material]
    slots = jnp.arange(P_SIZE, dtype=jnp.int32)
    device = slots // SLOT_DEV
    dev_x = device // (N_GY * N_GZ)
    dev_y = (device // N_GZ) % N_GY
    dev_z = device % N_GZ
    local_i = port_cell // (CY * CZ)
    local_j = (port_cell // CZ) % CY
    local_k = port_cell % CZ
    port_site = (local_i * NY + (dev_x * N_GY + dev_y) * CY + local_j) * NZ + dev_z * CZ + local_k
    electric = (e_field[0], e_field[1], e_field[2])
    magnetic = (h_field[0], h_field[1], h_field[2])
    states = pole_states
    for step in range(STEPS):
        volts = jnp.zeros((P_SIZE,), jnp.float32).at[port_owner].add(electric[2].reshape(-1)[port_site])
        ahead = (forward(electric[2], 1), forward(electric[1], 2), forward(electric[0], 2),
                 forward(electric[2], 0), forward(electric[1], 0), forward(electric[0], 1))
        magnetic = magnetic_update(electric, magnetic, ahead, decay_magn, curl_magn)
        die_volts = volts.reshape(NDIE, DP)
        states = pole_decay[:, :, None] * states + die_volts[:, None, :]
        current = direct * die_volts + jnp.einsum("dkrc,dkc->dr", residues, states, precision=lax.Precision.HIGHEST)
        source = jnp.zeros((NX * NY * NZ,), jnp.float32).at[port_site].add(current.reshape(-1)[port_owner])
        source = source.reshape(NX, NY, NZ)
        behind = (backward(magnetic[2], 1), backward(magnetic[1], 2), backward(magnetic[0], 2),
                  backward(magnetic[2], 0), backward(magnetic[1], 0), backward(magnetic[0], 1))
        electric = electric_update(electric, magnetic, behind, decay_elec, curl_elec, source)
    return jnp.stack(electric), jnp.stack(magnetic), states
```

```python
import jax
import jax.numpy as jnp
from jax import lax
from jax.experimental import pallas as pl
from jax.experimental.pallas import tpu as pltpu
from jax.sharding import PartitionSpec as P

ALL = ("gx", "gy", "gz")
F32 = jnp.float32
I32 = jnp.int32
LANES = 128
VMEM = pl.BlockSpec(memory_space=pltpu.VMEM)
SMEM = pl.BlockSpec(memory_space=pltpu.SMEM)
ANY = pl.BlockSpec(memory_space=pl.ANY)


def call(kernel, outs, ins, scratch=(), aliases=None, limit=16, specs_out=None):
    return pl.pallas_call(
        kernel,
        out_shape=tuple(jax.ShapeDtypeStruct(s, d) for s, d in outs),
        in_specs=list(ins),
        out_specs=tuple(specs_out) if specs_out else tuple(VMEM for _ in outs),
        scratch_shapes=list(scratch),
        input_output_aliases=aliases or {},
        compiler_params=pltpu.CompilerParams(vmem_limit_bytes=limit * 2**20),
    )


def shifted(value, axis, steps):
    count = lax.axis_size(axis)
    initial, last = (max(0, -steps), min(count, count - steps))
    return lax.ppermute(value, axis, [(source, source + steps) for source in range(initial, last)])


def lane_iota(shape):
    return lax.broadcasted_iota(I32, shape, len(shape) - 1)


def row_iota(shape):
    return lax.broadcasted_iota(I32, shape, 0)


def lookup(row, index):
    return jnp.take_along_axis(
        jnp.broadcast_to(row, index.shape), index, axis=1, mode="promise_in_bounds"
    )


def table_lookup(row, index):
    half = index.shape[1] // 2
    return jnp.concatenate([lookup(row, index[:, :half]), lookup(row, index[:, half:])], 1)


def load_tables(scratch, decay_ref, curl_ref):
    scratch[...] = jnp.zeros_like(scratch)
    scratch[0:2, 0:16] = decay_ref[...]
    scratch[2:4, 0:16] = curl_ref[...]


def cell_of(cell):
    return cell >> 14, (cell >> 8) & 63, cell & 255


def sample_rows(read_row, cell_ref, count):
    lane = lane_iota((1, LANES))

    def step(slot, acc):
        i, y, k = cell_of(cell_ref[slot])
        row = read_row(i, y)
        half = jnp.where(k >= LANES, row[:, LANES:], row[:, :LANES])
        moved = pltpu.roll(half, (slot - k) & (LANES - 1), 1)
        return jnp.where(lane == slot, moved, acc)

    return lax.fori_loop(0, count, step, jnp.zeros((1, LANES), F32), unroll=8)


def add_sources(field_ref, comp, cell_ref, values, count):
    lane = lane_iota((1, 2 * LANES))
    wide = jnp.broadcast_to(values, (8, LANES))

    def step(slot, carry):
        i, y, k = cell_of(cell_ref[slot])
        splat = lookup(wide[0:1], jnp.full((8, LANES), slot, I32))[0:1]
        both = jnp.concatenate([splat, splat], 1)
        row = field_ref[comp, i, pl.ds(y, 1), :]
        field_ref[comp, i, pl.ds(y, 1), :] = row - jnp.where(lane == k, both, 0.0)
        return carry

    lax.fori_loop(0, count, step, 0, unroll=4)


def electric_edges(e_ref, y_out, z_out):
    nx, ny = e_ref.shape[1], e_ref.shape[2]
    lane = lane_iota((ny, LANES))

    def step(i, acc):
        y_out[pl.ds(i, 1), :] = e_ref[0, i, 0:1, :]
        y_out[pl.ds(nx + i, 1), :] = e_ref[2, i, 0:1, :]
        for c in range(2):
            j = c * nx + i
            acc = jnp.where(lane == j, pltpu.roll(e_ref[c, i, :, 0:LANES], j, 1), acc)
        return acc

    z_out[...] = lax.fori_loop(0, nx, step, jnp.zeros((ny, LANES), F32))


def h_kernel(e_ref, h_ref, mat_ref, decay_ref, curl_ref, yh_ref, zh_ref, out_ref, yl_ref, zl_ref, tab):
    load_tables(tab, decay_ref, curl_ref)
    nx, ny, nz = mat_ref.shape
    row = row_iota((ny, nz))
    lane = lane_iota((ny, LANES))

    def from_y(value, halo):
        return jnp.where(row == ny - 1, halo, pltpu.roll(value, ny - 1, 0))

    def from_z(value, j):
        moved = pltpu.roll(value, nz - 1, 1)
        halo = pltpu.roll(zh_ref[...], (LANES - 1 - j) & (LANES - 1), 1)
        right = jnp.where(lane == LANES - 1, halo, moved[:, nz - LANES :])
        return jnp.concatenate([moved[:, : nz - LANES], right], 1)

    def step(i, acc):
        mat = mat_ref[i]
        decay = table_lookup(tab[1:2, :], mat)
        curl = table_lookup(tab[3:4, :], mat)
        ex, ey, ez = e_ref[0, i], e_ref[1, i], e_ref[2, i]
        after = jnp.minimum(i + 1, nx - 1)
        inside = i < nx - 1
        ey_x = jnp.where(inside, e_ref[1, after], 0.0)
        ez_x = jnp.where(inside, e_ref[2, after], 0.0)
        hx = decay * h_ref[0, i] - curl * (
            (from_y(ez, yh_ref[pl.ds(nx + i, 1), :]) - ez) - (from_z(ey, nx + i) - ey)
        )
        hy = decay * h_ref[1, i] - curl * ((from_z(ex, i) - ex) - (ez_x - ez))
        hz = decay * h_ref[2, i] - curl * (
            (ey_x - ey) - (from_y(ex, yh_ref[pl.ds(i, 1), :]) - ex)
        )
        out_ref[0, i] = hx
        out_ref[1, i] = hy
        out_ref[2, i] = hz
        yl_ref[pl.ds(i, 1), :] = hx[ny - 1 : ny, :]
        yl_ref[pl.ds(nx + i, 1), :] = hz[ny - 1 : ny, :]
        for c, value in enumerate((hx, hy)):
            j = c * nx + i
            moved = pltpu.roll(value[:, nz - LANES :], (j + 1) & (LANES - 1), 1)
            acc = jnp.where(lane == j, moved, acc)
        return acc

    zl_ref[...] = lax.fori_loop(0, nx, step, jnp.zeros((ny, LANES), F32))


def e_slab(i, e_ref, h_ref, mat_ref, yl_ref, zl_ref, tab):
    nx, ny, nz = mat_ref.shape
    row = row_iota((ny, nz))
    lane = lane_iota((ny, LANES))

    def from_y(value, halo):
        return jnp.where(row == 0, halo, pltpu.roll(value, 1, 0))

    def from_z(value, j):
        moved = pltpu.roll(value, 1, 1)
        halo = pltpu.roll(zl_ref[...], (LANES - j) & (LANES - 1), 1)
        left = jnp.where(lane == 0, halo, moved[:, :LANES])
        return jnp.concatenate([left, moved[:, LANES:]], 1)

    mat = mat_ref[i]
    decay = table_lookup(tab[0:1, :], mat)
    curl = table_lookup(tab[2:3, :], mat)
    hx, hy, hz = h_ref[0, i], h_ref[1, i], h_ref[2, i]
    before = jnp.maximum(i - 1, 0)
    inside = i > 0
    hy_x = jnp.where(inside, h_ref[1, before], 0.0)
    hz_x = jnp.where(inside, h_ref[2, before], 0.0)
    ex = decay * e_ref[0, i] + curl * (
        (hz - from_y(hz, yl_ref[pl.ds(nx + i, 1), :])) - (hy - from_z(hy, nx + i))
    )
    ey = decay * e_ref[1, i] + curl * ((hx - from_z(hx, i)) - (hz - hz_x))
    ez = decay * e_ref[2, i] + curl * (
        (hy - hy_x) - (hx - from_y(hx, yl_ref[pl.ds(i, 1), :]))
    )
    return ex, ey, ez


def e_kernel(e_ref, h_ref, mat_ref, decay_ref, curl_ref, yl_ref, zl_ref, cell_ref, out_ref, got_ref, tab):
    load_tables(tab, decay_ref, curl_ref)

    def step(i, carry):
        ex, ey, ez = e_slab(i, e_ref, h_ref, mat_ref, yl_ref, zl_ref, tab)
        out_ref[0, i] = ex
        out_ref[1, i] = ey
        out_ref[2, i] = ez
        return carry

    lax.fori_loop(0, mat_ref.shape[0], step, 0)
    got_ref[...] = sample_rows(
        lambda i, y: out_ref[2, i, pl.ds(y, 1), :], cell_ref, cell_ref.shape[0]
    )


def e_last_kernel(
    e_ref, h_ref, mat_ref, decay_ref, curl_ref, yl_ref, zl_ref, e_out, h_out, ez_ref, tab, buf, sem, h_sem
):
    load_tables(tab, decay_ref, curl_ref)
    nx = mat_ref.shape[0]
    h_copy = pltpu.make_async_copy(h_ref, h_out, h_sem)
    h_copy.start()

    def out_copy(i, c):
        return pltpu.make_async_copy(buf.at[c, i], e_out.at[c, i], sem.at[c])

    def step(i, carry):
        ex, ey, ez = e_slab(i, e_ref, h_ref, mat_ref, yl_ref, zl_ref, tab)
        buf[0, i] = ex
        buf[1, i] = ey
        ez_ref[i] = ez
        out_copy(i, 0).start()
        out_copy(i, 1).start()
        return carry

    lax.fori_loop(0, nx, step, 0)
    for c in range(2):
        pltpu.make_async_copy(buf.at[c], e_out.at[c], sem.at[c]).wait()
    h_copy.wait()


def finish_kernel(e_in, ez_ref, got_ref, curl_ref, cell_ref, e_out, work, sem):
    del e_in
    count = cell_ref.shape[0]
    work[0] = ez_ref[...]
    values = jnp.sum(got_ref[...], 0, keepdims=True) * curl_ref[...]
    add_sources(work, 0, cell_ref, values, count)
    copy = pltpu.make_async_copy(work.at[0], e_out.at[2], sem)
    copy.start()
    copy.wait()


def sample_kernel(e_ref, cell_ref, owner_ref, send_ref, y_out, z_out):
    count = cell_ref.shape[0]
    got = sample_rows(lambda i, y: e_ref[2, i, pl.ds(y, 1), :], cell_ref, count)
    owner = owner_ref[...].astype(F32)
    line = jnp.concatenate([got[:, :count], owner], 1)
    send_ref[...] = jnp.broadcast_to(line, send_ref.shape)
    electric_edges(e_ref, y_out, z_out)


def slot_kernel(mat_ref, curl_ref, cell_ref, cells_ref, line_ref, tab):
    count = cell_ref.shape[0]
    tab[...] = jnp.zeros_like(tab)
    tab[0:1, 0:16] = curl_ref[0:1, :]
    kinds = sample_rows(
        lambda i, y: mat_ref[i, pl.ds(y, 1), :].astype(F32), cell_ref, count
    )
    curl = lookup(tab[0:1, :], jnp.broadcast_to(kinds, (8, LANES)).astype(I32))[0:1]
    cells = cells_ref[...]
    cells = jnp.concatenate([cells, cells], 1)
    twin = jnp.zeros((1, LANES), F32)
    for r in range(1, count):
        twin = jnp.where(pltpu.roll(cells, r, 1) == cells, 1.0, twin)
    lane = lane_iota((1, LANES))
    line_ref[0:1, :] = jnp.where(lane < count, curl, 0.0)
    line_ref[1:2, :] = jnp.where(lane < count, cells.astype(F32), twin)


def across(value):
    return jnp.concatenate(
        [jnp.sum(value[h : h + LANES].T, 0, keepdims=True) for h in (0, LANES)], 1
    )


def residue_kernel(res_ref, decay_ref, state_ref, sum_ref, damp_ref, base_ref, line, acc):
    poles, rows, ports = res_ref.shape[1:]
    tiles = ports // LANES
    for k in range(poles):
        line[k : k + 1, :] = decay_ref[0, k] * state_ref[0, k : k + 1, :]
        line[poles + k : poles + k + 1, :] = decay_ref[0, k] * line[k : k + 1, :]

    def step(block, carry):
        at = pl.ds(pl.multiple_of(block * 8, 8), 8)
        one = jnp.zeros((8, LANES), F32)
        two = jnp.zeros((8, LANES), F32)
        for t in range(tiles):
            lanes = slice(t * LANES, (t + 1) * LANES)
            total = damp = None
            for k in range(poles):
                value = res_ref[0, k, at, lanes]
                one = one + value * line[k : k + 1, lanes]
                two = two + value * line[poles + k : poles + k + 1, lanes]
                scaled = decay_ref[0, k] * value
                total = value if total is None else total + value
                damp = scaled if damp is None else damp + scaled
            sum_ref[at, lanes] = total
            damp_ref[at, lanes] = damp
        acc[0, at, :] = one
        acc[1, at, :] = two
        return carry

    lax.fori_loop(0, rows // 8, step, 0)
    base_ref[0:1, :] = across(acc[0])
    base_ref[1:2, :] = across(acc[1])


def apply(mat_ref, volts):
    total = None
    for t in range(volts.shape[0]):
        part = mat_ref[:, t * LANES : (t + 1) * LANES] * volts[t : t + 1, :]
        total = part if total is None else total + part
    return total


def fetch(tab_ref, rows, lanes):
    acc = jnp.zeros(lanes.shape, F32)
    for r in range(tab_ref.shape[0]):
        acc = jnp.where(rows == r, lookup(tab_ref[r : r + 1, :], lanes), acc)
    return acc


def own_ports(volts_ref, index_x):
    return jnp.concatenate(
        [volts_ref[pl.ds(2 * index_x + h, 1), :] for h in range(2)], 1
    )


def first_kernel(recv_ref, sum_ref, base_ref, direct_ref, where_ref, own_ref, at_ref, volts_ref, cur_ref, tab):
    index_x, index_y, die = where_ref[0], where_ref[1], where_ref[2]
    half = lane_iota((64, LANES)) < 64
    even = recv_ref[pl.ds(0, 64, stride=2), :]
    odd = recv_ref[pl.ds(1, 64, stride=2), :]
    tab[...] = jnp.where(half, even, pltpu.roll(odd, 64, 1))
    owner = jnp.where(half, pltpu.roll(even, 64, 1), odd).astype(I32)
    own_ref[...] = owner
    high, low = owner >> 7, owner & (LANES - 1)
    port = die * 8 + row_iota((8, LANES))
    lane = lane_iota((8, LANES)).astype(F32)
    spot = row_iota((LANES, LANES))
    found = jnp.zeros((16, LANES), F32)
    for r in range(0, 64, 2):
        picks, marks = [], []
        for q in (r, r + 1):
            mine = high[q : q + 1, :] == port
            picks.append(
                jnp.concatenate(
                    [jnp.where(mine, float(q), 0.0), jnp.where(mine, lane, 0.0)], 0
                ).astype(jnp.bfloat16)
            )
            marks.append(
                jnp.where(low[q : q + 1, :] == spot, 1.0, 0.0).astype(jnp.bfloat16)
            )
        found = found + lax.dot_general(
            jnp.concatenate(picks, 1),
            jnp.concatenate(marks, 1),
            (((1,), (1,)), ((), ())),
            preferred_element_type=F32,
        )
    found = found.astype(I32)
    rows, lanes = found[0:8], found[8:16]
    at_ref[0] = rows
    at_ref[1] = lanes
    volts = fetch(tab, rows, lanes)
    volts_ref[...] = volts
    current = across(apply(sum_ref, volts)) + base_ref[0:1, :]
    through = direct_ref[...] * own_ports(volts_ref, index_x)
    cur_ref[...] = current + jnp.where(index_y == 0, through, 0.0)


def pack_kernel(got_ref, line_ref, cur_ref, send_ref):
    lane = lane_iota((1, LANES))
    first = jnp.where(lane < 64, got_ref[...], pltpu.roll(line_ref[0:1, :], 64, 1))
    shape = (8, LANES)
    turn = row_iota(shape) & 3
    block = jnp.where(turn == 0, first, jnp.where(turn == 3, line_ref[1:2, :], 0.0))
    block = jnp.where(turn == 1, cur_ref[:, :LANES], block)
    block = jnp.where(turn == 2, cur_ref[:, LANES:], block)

    def step(n, carry):
        send_ref[pl.ds(pl.multiple_of(n * 8, 8), 8), :] = block
        return carry

    lax.fori_loop(0, send_ref.shape[0] // 8, step, 0, unroll=8)


def turn64(value, r):
    lane = lane_iota(value.shape) & 63
    return jnp.where(
        lane >= r, pltpu.roll(value, r, 1), pltpu.roll(value, (r + 64) & (LANES - 1), 1)
    )


def second_kernel(
    recv_ref, own_ref, at_ref, volts_ref, sum_ref, damp_ref, base_ref, direct_ref,
    decay_ref, state_ref, owner_ref, where_ref,
    states_ref, send_ref, mine_ref,
    cur_tab, ez_tab, curl_tab, shared, next_ref,
):
    index_x, index_y, die = where_ref[0], where_ref[1], where_ref[2]
    half = lane_iota((64, LANES)) < 64
    for gx in range(4):
        for h in range(2):
            total = None
            for gy in range(4):
                part = recv_ref[pl.ds((gx * 4 + gy) * 32 + 1 + h, 8, stride=4), :]
                total = part if total is None else total + part
            cur_tab[pl.ds(gx * 2 + h, 8, stride=8), :] = total
    even = recv_ref[pl.ds(0, 64, stride=8), :]
    odd = recv_ref[pl.ds(4, 64, stride=8), :]
    ez_tab[...] = jnp.where(half, even, pltpu.roll(odd, 64, 1))
    curl_tab[...] = jnp.where(half, pltpu.roll(even, 64, 1), odd)
    rows, lanes = at_ref[0], at_ref[1]
    shared[0:8, :] = cur_tab[pl.ds(pl.multiple_of(die * 8, 8), 8), :]

    even = recv_ref[pl.ds(3, 64, stride=8), :]
    odd = recv_ref[pl.ds(7, 64, stride=8), :]
    flags = jnp.where(half, 0.0, jnp.maximum(even, odd))

    @pl.when(jnp.max(flags) > 0.5)
    def _():
        cells = jnp.where(half, even, pltpu.roll(odd, 64, 1))
        owner = own_ref[...]
        high, low = owner >> 7, owner & (LANES - 1)

        def pick(r, acc):
            return jnp.where(high == r, lookup(cur_tab[pl.ds(r, 1), :], low), acc)

        slots = lax.fori_loop(0, 64, pick, jnp.zeros((64, LANES), F32))

        def gather(r, acc):
            same = turn64(cells, r) == cells
            return acc + jnp.where(same, turn64(slots, r), 0.0)

        shared[8:72, :] = lax.fori_loop(1, 64, gather, slots)
        shared[0:8, :] = fetch(shared.at[8:72], rows, lanes)

    volts = fetch(ez_tab, rows, lanes) - fetch(curl_tab, rows, lanes) * shared[0:8, :]
    next_ref[...] = volts
    current = across(apply(sum_ref, volts) + apply(damp_ref, volts_ref[...])) + base_ref[1:2, :]
    through = direct_ref[...] * own_ports(next_ref, index_x)
    current = current + jnp.where(index_y == 0, through, 0.0)
    owner = own_ref[...]
    low = owner & (LANES - 1)
    picked = jnp.where(
        ((owner >> 7) & 1) == 1, lookup(current[:, LANES:], low), lookup(current[:, :LANES], low)
    )
    picked = jnp.where((owner >> 8) == die * 4 + index_x, picked, 0.0)
    send_ref[pl.ds(0, 64, stride=2), :] = jnp.where(half, picked, 0.0)
    send_ref[pl.ds(1, 64, stride=2), :] = jnp.where(half, pltpu.roll(picked, 64, 1), 0.0)
    for k in range(states_ref.shape[1]):
        fade = decay_ref[0, k]
        for t in range(8):
            at = slice(t * LANES, (t + 1) * LANES)
            old = fade * state_ref[0, k : k + 1, at] + volts_ref[t : t + 1, :]
            states_ref[0, k : k + 1, at] = fade * old + volts[t : t + 1, :]
    owner = jnp.concatenate([owner_ref[...], owner_ref[...]], 1)
    owner = jnp.broadcast_to(owner, (8, LANES))
    mine_ref[...] = fetch(cur_tab, owner >> 7, owner & (LANES - 1))[0:1]


def source_kernel(e_in, mine_ref, line_ref, cell_ref, e_ref, y_out, z_out):
    del e_in
    add_sources(e_ref, 2, cell_ref, mine_ref[...] * line_ref[0:1, :], cell_ref.shape[0])
    electric_edges(e_ref, y_out, z_out)


def body(
    e_field, h_field, material, decay_table, curl_table, residues, pole_decay,
    pole_states, direct, port_cell, port_owner,
):
    field, (nx, ny, nz) = e_field.shape, material.shape
    slots = port_cell.shape[0]
    devices = lax.axis_size(ALL)
    rows, ports = residues.shape[2:]
    where = jnp.stack([lax.axis_index(name) for name in ALL]).astype(I32)
    y_edge, z_edge = ((2 * nx, nz), F32), ((ny, LANES), F32)
    table = pltpu.VMEM((8, LANES), F32)
    cells = port_cell.reshape(1, slots)
    owners = port_owner.reshape(1, slots)

    def edges_back(y, z):
        return shifted(y, ("gx", "gy"), -1), shifted(z, "gz", -1)

    def edges_on(y, z):
        return shifted(y, ("gx", "gy"), 1), shifted(z, "gz", 1)

    def magnetic(electric, old, y, z):
        return call(
            h_kernel, ((field, F32), y_edge, z_edge), (VMEM,) * 7, (table,)
        )(electric, old, material, decay_table, curl_table, y, z)

    send, y, z = call(
        sample_kernel, (((devices, LANES), F32), y_edge, z_edge), (VMEM, SMEM, VMEM)
    )(e_field, port_cell, owners)
    y, z = edges_back(y, z)
    recv = lax.all_to_all(send, ALL, 0, 0, tiled=True)
    sums, damped, base = call(
        residue_kernel,
        (((rows, ports), F32), ((rows, ports), F32), ((8, rows), F32)),
        (VMEM, SMEM, VMEM),
        (pltpu.VMEM((8, ports), F32), pltpu.VMEM((2, rows, LANES), F32)),
    )(residues, pole_decay, pole_states)
    (line,) = call(slot_kernel, (((8, LANES), F32),), (VMEM, VMEM, SMEM, VMEM), (table,))(
        material, curl_table, port_cell, cells
    )
    h_one, y, z = magnetic(e_field, h_field, y, z)
    y, z = edges_on(y, z)
    own, at, volts, current = call(
        first_kernel,
        (((64, LANES), I32), ((2, 8, LANES), I32), ((8, LANES), F32), ((1, rows), F32)),
        (VMEM, VMEM, VMEM, VMEM, SMEM),
        (pltpu.VMEM((64, LANES), F32),),
    )(recv, sums, base, direct, where)
    e_one, got = call(
        e_kernel, ((field, F32), ((1, LANES), F32)), (VMEM,) * 7 + (SMEM,), (table,)
    )(e_field, h_one, material, decay_table, curl_table, y, z, port_cell)
    (send,) = call(pack_kernel, (((4 * devices, LANES), F32),), (VMEM,) * 3)(got, line, current)
    recv = lax.all_to_all(send, ALL, 0, 0, tiled=True)
    states, send, mine = call(
        second_kernel,
        ((pole_states.shape, F32), ((devices, LANES), F32), ((1, LANES), F32)),
        (VMEM,) * 8 + (SMEM, VMEM, VMEM, SMEM),
        (
            pltpu.VMEM((64, LANES), F32),
            pltpu.VMEM((64, LANES), F32),
            pltpu.VMEM((64, LANES), F32),
            pltpu.VMEM((72, LANES), F32),
            pltpu.VMEM((8, LANES), F32),
        ),
    )(recv, own, at, volts, sums, damped, base, direct, pole_decay, pole_states, owners, where)
    e_one, y, z = call(
        source_kernel, ((field, F32), y_edge, z_edge), (VMEM, VMEM, VMEM, SMEM), aliases={0: 0}
    )(e_one, mine, line, port_cell)
    y, z = edges_back(y, z)
    recv = lax.all_to_all(send, ALL, 0, 0, tiled=True)
    h_two, y, z = magnetic(e_one, h_one, y, z)
    y, z = edges_on(y, z)
    e_out, h_out, ez = call(
        e_last_kernel,
        ((field, F32), (field, F32), (field[1:], F32)),
        (VMEM,) * 7,
        (
            table,
            pltpu.VMEM((2,) + field[1:], F32),
            pltpu.SemaphoreType.DMA((2,)),
            pltpu.SemaphoreType.DMA,
        ),
        specs_out=(ANY, ANY, VMEM),
    )(e_one, h_two, material, decay_table, curl_table, y, z)
    (e_out,) = call(
        finish_kernel,
        ((field, F32),),
        (ANY, VMEM, VMEM, VMEM, SMEM),
        (pltpu.VMEM((1,) + field[1:], F32), pltpu.SemaphoreType.DMA),
        aliases={0: 0},
        specs_out=(ANY,),
    )(e_out, ez, recv, line[0:1], port_cell)
    return e_out, h_out, states


def solution(mesh):
    return jax.shard_map(
        body,
        mesh=mesh,
        in_specs=(
            P(None, None, ("gx", "gy"), "gz"),
            P(None, None, ("gx", "gy"), "gz"),
            P(None, ("gx", "gy"), "gz"),
            P(),
            P(),
            P("gz", "gy", "gx", None),
            P("gz", "gy"),
            P("gz", "gy", None),
            P("gz", "gx"),
            P(("gx", "gy", "gz")),
            P(("gx", "gy", "gz")),
        ),
        out_specs=(
            P(None, None, ("gx", "gy"), "gz"),
            P(None, None, ("gx", "gy"), "gz"),
            P("gz", "gy", None),
        ),
        check_vma=False,
    )
```

```python
import jax
import jax.numpy as jnp
from jax import lax
from jax.experimental import pallas as pl
from jax.experimental.pallas import tpu as pltpu
from jax.sharding import PartitionSpec as P


ALL = ("gx", "gy", "gz")
F32 = jnp.float32
I32 = jnp.int32
LANES = 128
UNROLL = 2
VMEM = pl.BlockSpec(memory_space=pltpu.VMEM)
SMEM = pl.BlockSpec(memory_space=pltpu.SMEM)
HBM = pl.BlockSpec(memory_space=pltpu.HBM)


def call(kernel, outs, ins, scratch=(), aliases=None, limit=16, specs_out=None):
    return pl.pallas_call(
        kernel,
        out_shape=tuple(jax.ShapeDtypeStruct(s, d) for s, d in outs),
        in_specs=list(ins),
        out_specs=tuple(specs_out) if specs_out else tuple(VMEM for _ in outs),
        scratch_shapes=list(scratch),
        input_output_aliases=aliases or {},
        compiler_params=pltpu.CompilerParams(vmem_limit_bytes=limit * 2**20),
    )


def in_hbm(value):
    return pltpu.with_memory_space_constraint(value, pltpu.HBM)


def shifted(value, axis, steps):
    count = lax.axis_size(axis)
    initial, last = (max(0, -steps), min(count, count - steps))
    return lax.ppermute(value, axis, [(source, source + steps) for source in range(initial, last)])


def lane_iota(shape):
    return lax.broadcasted_iota(I32, shape, len(shape) - 1)


def row_iota(shape):
    return lax.broadcasted_iota(I32, shape, 0)


def lookup(row, index):
    return jnp.take_along_axis(
        jnp.broadcast_to(row, index.shape), index, axis=1, mode="promise_in_bounds"
    )


def table_lookup(row, index):
    half = index.shape[1] // 2
    return jnp.concatenate([lookup(row, index[:, :half]), lookup(row, index[:, half:])], 1)


def tree_lookup(entries, bits):
    for bit in bits:
        entries = [
            jnp.where(bit, odd, even) for even, odd in zip(entries[0::2], entries[1::2])
        ]
    return entries[0]


def load_tables(scratch, decay_ref, curl_ref):
    scratch[...] = jnp.zeros_like(scratch)
    scratch[0:2, 0:16] = decay_ref[...]
    scratch[2:4, 0:16] = curl_ref[...]


def cell_of(cell):
    return cell >> 14, (cell >> 8) & 63, cell & 255


def sample_rows(read_row, cell_ref, count):
    lane = lane_iota((1, LANES))

    def step(slot, acc):
        i, y, k = cell_of(cell_ref[slot])
        row = read_row(i, y)
        half = jnp.where(k >= LANES, row[:, LANES:], row[:, :LANES])
        moved = pltpu.roll(half, (slot - k) & (LANES - 1), 1)
        return jnp.where(lane == slot, moved, acc)

    return lax.fori_loop(0, count, step, jnp.zeros((1, LANES), F32), unroll=count)


def split3(value):
    high = value.astype(jnp.bfloat16)
    rest = value - high.astype(F32)
    middle = rest.astype(jnp.bfloat16)
    return high, middle, (rest - middle.astype(F32)).astype(jnp.bfloat16)


def add_sources(field_ref, lead, cell_ref, values, same_ref, mark_ref, work):
    count = cell_ref.shape[0]
    scaled = same_ref[...] * values[:, :count]
    marks = mark_ref[...].astype(jnp.bfloat16)
    total = None
    for part in split3(scaled):
        product = jnp.dot(part, marks, preferred_element_type=F32)
        total = product if total is None else total + product
    work[...] = total
    for slot in range(count):
        i, y, _ = cell_of(cell_ref[slot])
        row = field_ref[lead + (i, pl.ds(y, 1))]
        work[slot : slot + 1, :] = row - work[slot : slot + 1, :]
    for slot in range(count):
        i, y, _ = cell_of(cell_ref[slot])
        field_ref[lead + (i, pl.ds(y, 1))] = work[slot : slot + 1, :]


def electric_edges(nx, first_row, first_tile, y_out, z_out):
    ny = z_out.shape[0]
    lane = lane_iota((ny, LANES))

    def step(i, acc):
        y_out[pl.ds(i, 1), :] = first_row(0, i)
        y_out[pl.ds(nx + i, 1), :] = first_row(1, i)
        for c in range(2):
            j = c * nx + i
            acc = jnp.where(lane == j, pltpu.roll(first_tile(c, i), j, 1), acc)
        return acc

    z_out[...] = lax.fori_loop(0, nx, step, jnp.zeros((ny, LANES), F32), unroll=6)


def factor_kernel(
    mat_in, e_in, h_in, decay_ref, curl_ref, curl_sm,
    magn_ref, elec_ref, e_ref, h_ref, tab, mat_ref, mat_sem, field_sem,
):
    parts = mat_sem.shape[0]
    size = mat_ref.shape[0] // parts
    copies = []
    for p in range(parts):
        at = slice(p * size, (p + 1) * size)
        copies.append(pltpu.make_async_copy(mat_in.at[at], mat_ref.at[at], mat_sem.at[p]))
    fields = [
        pltpu.make_async_copy(e_in, e_ref, field_sem.at[0]),
        pltpu.make_async_copy(h_in, h_ref, field_sem.at[1]),
    ]
    for copy in copies + fields:
        copy.start()
    load_tables(tab, decay_ref, curl_ref)

    def step(i, carry):
        mat = mat_ref[i]
        bits = [(mat & (1 << b)) != 0 for b in range(4)]
        magn_ref[0, i] = table_lookup(tab[1:2, :], mat)
        magn_ref[1, i] = table_lookup(tab[3:4, :], mat)
        elec_ref[0, i] = table_lookup(tab[0:1, :], mat)
        elec_ref[1, i] = tree_lookup([curl_sm[0, n] for n in range(16)], bits)
        return carry

    for p in range(parts):
        copies[p].wait()
        lax.fori_loop(p * size, (p + 1) * size, step, 0, unroll=UNROLL)
    for copy in fields:
        copy.wait()


def h_kernel(e_ref, h_ref, magn_ref, yh_ref, zh_ref, out_ref, yl_ref, zl_ref):
    def factors(i):
        return magn_ref[0, i], magn_ref[1, i]

    acc = jnp.zeros(zl_ref.shape, F32)
    zl_ref[...] = h_update(
        factors, e_ref, h_ref, yh_ref, zh_ref, out_ref, yl_ref, acc, 0, e_ref.shape[1]
    )


def h_update(factors, e_ref, h_ref, yh_ref, zh_ref, out_ref, yl_ref, acc, begin, end):
    nx, ny, nz = e_ref.shape[1:]
    row = row_iota((ny, nz))
    lane = lane_iota((ny, LANES))

    def from_y(value, halo):
        return jnp.where(row == ny - 1, halo, pltpu.roll(value, ny - 1, 0))

    def from_z(value, j):
        moved = pltpu.roll(value, nz - 1, 1)
        halo = pltpu.roll(zh_ref[...], (LANES - 1 - j) & (LANES - 1), 1)
        right = jnp.where(lane == LANES - 1, halo, moved[:, nz - LANES :])
        return jnp.concatenate([moved[:, : nz - LANES], right], 1)

    def step(i, acc):
        decay, curl = factors(i)
        ex, ey, ez = e_ref[0, i], e_ref[1, i], e_ref[2, i]
        after = jnp.minimum(i + 1, nx - 1)
        inside = i < nx - 1
        ey_x = jnp.where(inside, e_ref[1, after], 0.0)
        ez_x = jnp.where(inside, e_ref[2, after], 0.0)
        hx = decay * h_ref[0, i] - curl * (
            (from_y(ez, yh_ref[pl.ds(nx + i, 1), :]) - ez) - (from_z(ey, nx + i) - ey)
        )
        hy = decay * h_ref[1, i] - curl * ((from_z(ex, i) - ex) - (ez_x - ez))
        hz = decay * h_ref[2, i] - curl * (
            (ey_x - ey) - (from_y(ex, yh_ref[pl.ds(i, 1), :]) - ex)
        )
        out_ref[0, i] = hx
        out_ref[1, i] = hy
        out_ref[2, i] = hz
        yl_ref[pl.ds(i, 1), :] = hx[ny - 1 : ny, :]
        yl_ref[pl.ds(nx + i, 1), :] = hz[ny - 1 : ny, :]
        for c, value in enumerate((hx, hy)):
            j = c * nx + i
            moved = pltpu.roll(value[:, nz - LANES :], (j + 1) & (LANES - 1), 1)
            acc = jnp.where(lane == j, moved, acc)
        return acc

    return lax.fori_loop(begin, end, step, acc, unroll=UNROLL)


def e_slab(i, e_ref, h_ref, elec_ref, yl_ref, zl_ref):
    nx, ny, nz = e_ref.shape[1:]
    row = row_iota((ny, nz))
    lane = lane_iota((ny, LANES))

    def from_y(value, halo):
        return jnp.where(row == 0, halo, pltpu.roll(value, 1, 0))

    def from_z(value, j):
        moved = pltpu.roll(value, 1, 1)
        halo = pltpu.roll(zl_ref[...], (LANES - j) & (LANES - 1), 1)
        left = jnp.where(lane == 0, halo, moved[:, :LANES])
        return jnp.concatenate([left, moved[:, LANES:]], 1)

    decay, curl = elec_ref[0, i], elec_ref[1, i]
    hx, hy, hz = h_ref[0, i], h_ref[1, i], h_ref[2, i]
    before = jnp.maximum(i - 1, 0)
    inside = i > 0
    hy_x = jnp.where(inside, h_ref[1, before], 0.0)
    hz_x = jnp.where(inside, h_ref[2, before], 0.0)
    ex = decay * e_ref[0, i] + curl * (
        (hz - from_y(hz, yl_ref[pl.ds(nx + i, 1), :])) - (hy - from_z(hy, nx + i))
    )
    ey = decay * e_ref[1, i] + curl * ((hx - from_z(hx, i)) - (hz - hz_x))
    ez = decay * e_ref[2, i] + curl * (
        (hy - hy_x) - (hx - from_y(hx, yl_ref[pl.ds(i, 1), :]))
    )
    return ex, ey, ez


def e_kernel(e_ref, h_ref, elec_ref, yl_ref, zl_ref, cell_ref, out_ref, got_ref):
    def step(i, carry):
        ex, ey, ez = e_slab(i, e_ref, h_ref, elec_ref, yl_ref, zl_ref)
        out_ref[0, i] = ex
        out_ref[1, i] = ey
        out_ref[2, i] = ez
        return carry

    lax.fori_loop(0, e_ref.shape[1], step, 0, unroll=UNROLL)
    got_ref[...] = sample_rows(
        lambda i, y: out_ref[2, i, pl.ds(y, 1), :], cell_ref, cell_ref.shape[0]
    )


def e_last_kernel(
    e_ref, h_ref, elec_ref, yl_ref, zl_ref, e_out, h_out, ez_ref, buf, sem, h_sem
):
    nx = e_ref.shape[1]
    h_copy = pltpu.make_async_copy(h_ref, h_out, h_sem)
    h_copy.start()

    def out_copy(i, c):
        return pltpu.make_async_copy(buf.at[c, i], e_out.at[c, i], sem.at[c])

    def step(i, carry):
        ex, ey, ez = e_slab(i, e_ref, h_ref, elec_ref, yl_ref, zl_ref)
        buf[0, i] = ex
        buf[1, i] = ey
        ez_ref[i] = ez
        out_copy(i, 0).start()
        out_copy(i, 1).start()
        return carry

    lax.fori_loop(0, nx, step, 0, unroll=UNROLL)
    for c in range(2):
        pltpu.make_async_copy(buf.at[c], e_out.at[c], sem.at[c]).wait()
    h_copy.wait()


def finish_kernel(
    e_in, ez_in, got_ref, line_ref, cell_ref, same_ref, mark_ref, e_out, ez_ref, work, sem
):
    del e_in, ez_in
    values = jnp.sum(got_ref[...], 0, keepdims=True) * line_ref[0:1, :]
    add_sources(ez_ref, (), cell_ref, values, same_ref, mark_ref, work)
    copy = pltpu.make_async_copy(ez_ref, e_out.at[2], sem)
    copy.start()
    copy.wait()


def sample_kernel(
    e_ref, cell_in, owner_in, send_ref, y_out, z_out,
    cell_ref, owner_ref, slabs, rows, tiles, sems,
):
    count, nx = cell_in.shape[0], e_ref.shape[1]
    cell_copy = pltpu.make_async_copy(cell_in, cell_ref, sems.at[0])
    cell_copy.start()
    owner_copy = pltpu.make_async_copy(owner_in, owner_ref, sems.at[1])
    owner_copy.start()
    y_copies = [
        pltpu.make_async_copy(e_ref.at[2 * c, :, 0:8], rows.at[c], sems.at[4 + c])
        for c in range(2)
    ]
    for copy in y_copies:
        copy.start()
    z_copy = pltpu.make_async_copy(e_ref.at[0:2, :, :, 0:LANES], tiles, sems.at[3])
    z_copy.start()
    cell_copy.wait()
    for slot in range(count):
        i, y, _ = cell_of(cell_ref[slot])
        block = pl.ds(pl.multiple_of((y >> 3) << 3, 8), 8)
        pltpu.make_async_copy(e_ref.at[2, i, block], slabs.at[slot], sems.at[2]).start()
    owner_copy.wait()
    pltpu.make_async_copy(slabs, slabs, sems.at[2]).wait()
    lane = lane_iota((1, LANES))
    got = jnp.zeros((1, LANES), F32)
    for slot in range(count):
        _, y, k = cell_of(cell_ref[slot])
        row = slabs[slot, pl.ds(y & 7, 1), :]
        half = jnp.where(k >= LANES, row[:, LANES:], row[:, :LANES])
        got = jnp.where(lane == slot, pltpu.roll(half, (slot - k) & (LANES - 1), 1), got)
    owner = owner_ref[...].astype(F32)
    line = jnp.concatenate([got[:, :count], owner], 1)
    send_ref[...] = jnp.broadcast_to(line, send_ref.shape)
    for copy in y_copies:
        copy.wait()
    z_copy.wait()
    electric_edges(
        nx, lambda c, i: rows[c, i, 0:1, :], lambda c, i: tiles[c, i], y_out, z_out
    )


def slot_kernel(mat_ref, curl_ref, cell_ref, cells_ref, line_ref, same_ref, mark_ref, tab):
    count = cell_ref.shape[0]
    tab[...] = jnp.zeros_like(tab)
    tab[0:1, 0:16] = curl_ref[0:1, :]
    kinds = sample_rows(
        lambda i, y: mat_ref[i, pl.ds(y, 1), :].astype(F32), cell_ref, count
    )
    curl = lookup(tab[0:1, :], jnp.broadcast_to(kinds, (8, LANES)).astype(I32))[0:1]
    cells = cells_ref[...]
    cells = jnp.concatenate([cells, cells], 1)
    twin = jnp.zeros((1, LANES), F32)
    for r in range(1, count):
        twin = jnp.where(pltpu.roll(cells, r, 1) == cells, 1.0, twin)
    lane = lane_iota((1, LANES))
    line_ref[0:1, :] = jnp.where(lane < count, curl, 0.0)
    wide = lane_iota((1, mark_ref.shape[1]))
    grid_row = cells_ref[...] >> 8
    for slot in range(count):
        cell = cell_ref[slot]
        same_ref[slot : slot + 1, :] = jnp.where(grid_row == (cell >> 8), 1.0, 0.0)
        mark_ref[slot : slot + 1, :] = jnp.where(wide == (cell & 255), 1.0, 0.0)
    line_ref[1:2, :] = jnp.where(lane < count, cells.astype(F32), twin)


def across(value):
    return jnp.concatenate(
        [jnp.sum(value[h : h + LANES].T, 0, keepdims=True) for h in (0, LANES)], 1
    )


def residue_kernel(res_ref, decay_ref, state_ref, sum_ref, damp_ref, base_ref, line, acc):
    poles, rows, ports = res_ref.shape[1:]
    tiles = ports // LANES
    for k in range(poles):
        line[k : k + 1, :] = decay_ref[0, k] * state_ref[0, k : k + 1, :]
        line[poles + k : poles + k + 1, :] = decay_ref[0, k] * line[k : k + 1, :]

    def step(block, carry):
        at = pl.ds(pl.multiple_of(block * 8, 8), 8)
        one = jnp.zeros((8, LANES), F32)
        two = jnp.zeros((8, LANES), F32)
        for t in range(tiles):
            lanes = slice(t * LANES, (t + 1) * LANES)
            total = damp = None
            for k in range(poles):
                value = res_ref[0, k, at, lanes]
                one = one + value * line[k : k + 1, lanes]
                two = two + value * line[poles + k : poles + k + 1, lanes]
                scaled = decay_ref[0, k] * value
                total = value if total is None else total + value
                damp = scaled if damp is None else damp + scaled
            sum_ref[at, lanes] = total
            damp_ref[at, lanes] = damp
        acc[0, at, :] = one
        acc[1, at, :] = two
        return carry

    lax.fori_loop(0, rows // 8, step, 0)
    base_ref[0:1, :] = across(acc[0])
    base_ref[1:2, :] = across(acc[1])


def apply(mat_ref, volts):
    total = None
    for t in range(volts.shape[0]):
        part = mat_ref[:, t * LANES : (t + 1) * LANES] * volts[t : t + 1, :]
        total = part if total is None else total + part
    return total


def fetch(tab_ref, rows, lanes):
    acc = jnp.zeros(lanes.shape, F32)
    for r in range(tab_ref.shape[0]):
        acc = jnp.where(rows == r, lookup(tab_ref[r : r + 1, :], lanes), acc)
    return acc


def own_ports(volts_ref, index_x):
    return jnp.concatenate(
        [volts_ref[pl.ds(2 * index_x + h, 1), :] for h in range(2)], 1
    )


def first_kernel(recv_ref, sum_ref, base_ref, direct_ref, own_ref, at_ref, volts_ref, cur_ref, tab):
    index_x, index_y, die = (lax.axis_index(name) for name in ALL)
    half = lane_iota((64, LANES)) < 64
    even = recv_ref[pl.ds(0, 64, stride=2), :]
    odd = recv_ref[pl.ds(1, 64, stride=2), :]
    tab[...] = jnp.where(half, even, pltpu.roll(odd, 64, 1))
    owner = jnp.where(half, pltpu.roll(even, 64, 1), odd).astype(I32)
    own_ref[...] = owner
    high, low = owner >> 7, owner & (LANES - 1)
    port = die * 8 + row_iota((8, LANES))
    lane = lane_iota((8, LANES)).astype(F32)
    spot = row_iota((LANES, LANES))
    found = jnp.zeros((16, LANES), F32)
    for r in range(0, 64, 2):
        picks, marks = [], []
        for q in (r, r + 1):
            mine = high[q : q + 1, :] == port
            picks.append(
                jnp.concatenate(
                    [jnp.where(mine, float(q), 0.0), jnp.where(mine, lane, 0.0)], 0
                ).astype(jnp.bfloat16)
            )
            marks.append(
                jnp.where(low[q : q + 1, :] == spot, 1.0, 0.0).astype(jnp.bfloat16)
            )
        found = found + lax.dot_general(
            jnp.concatenate(picks, 1),
            jnp.concatenate(marks, 1),
            (((1,), (1,)), ((), ())),
            preferred_element_type=F32,
        )
    found = found.astype(I32)
    rows, lanes = found[0:8], found[8:16]
    at_ref[0] = rows
    at_ref[1] = lanes
    volts = fetch(tab, rows, lanes)
    volts_ref[...] = volts
    current = across(apply(sum_ref, volts)) + base_ref[0:1, :]
    through = direct_ref[...] * own_ports(volts_ref, index_x)
    cur_ref[...] = current + jnp.where(index_y == 0, through, 0.0)


def pack_kernel(got_ref, line_ref, cur_ref, send_ref):
    lane = lane_iota((1, LANES))
    first = jnp.where(lane < 64, got_ref[...], pltpu.roll(line_ref[0:1, :], 64, 1))
    shape = (8, LANES)
    turn = row_iota(shape) & 3
    block = jnp.where(turn == 0, first, jnp.where(turn == 3, line_ref[1:2, :], 0.0))
    block = jnp.where(turn == 1, cur_ref[:, :LANES], block)
    block = jnp.where(turn == 2, cur_ref[:, LANES:], block)

    def step(n, carry):
        send_ref[pl.ds(pl.multiple_of(n * 8, 8), 8), :] = block
        return carry

    lax.fori_loop(0, send_ref.shape[0] // 8, step, 0, unroll=8)


def turn64(value, r, lane):
    return jnp.where(
        (lane & 63) >= r, pltpu.roll(value, r, 1), pltpu.roll(value, (r + 64) & (LANES - 1), 1)
    )


def second_kernel(
    recv_ref, cur_tab, own_ref, at_ref, volts_ref, sum_ref, damp_ref, base_ref, direct_ref,
    decay_ref, state_ref,
    states_ref, send_ref,
    ez_tab, curl_tab, cell_tab, shared, cur8, next_ref,
):
    index_x, index_y, die = (lax.axis_index(name) for name in ALL)
    half = lane_iota((64, LANES)) < 64
    even = recv_ref[pl.ds(0, 64, stride=8), :]
    odd = recv_ref[pl.ds(4, 64, stride=8), :]
    ez_tab[...] = jnp.where(half, even, pltpu.roll(odd, 64, 1))
    curl_tab[...] = jnp.where(half, pltpu.roll(even, 64, 1), odd)
    rows, lanes = at_ref[0], at_ref[1]
    cur8[...] = cur_tab[pl.ds(pl.multiple_of(die * 8, 8), 8), :]

    even = recv_ref[pl.ds(3, 64, stride=8), :]
    odd = recv_ref[pl.ds(7, 64, stride=8), :]
    flags = jnp.where(half, 0.0, jnp.maximum(even, odd))

    @pl.when(jnp.max(flags) > 0.5)
    def _():
        cell_tab[...] = jnp.where(half, even, pltpu.roll(odd, 64, 1))
        shared[...] = jnp.zeros_like(shared)
        number = row_iota((64, LANES)).astype(F32)
        line = lane_iota((1, LANES))

        def one_row(left):
            at = jnp.max(left).astype(I32) - 1
            cells = cell_tab[pl.ds(at, 1), :]
            owner = jnp.broadcast_to(own_ref[pl.ds(at, 1), :], (8, LANES))
            slots = fetch(cur_tab, owner >> 7, owner & (LANES - 1))[0:1]
            total = jnp.zeros((1, LANES), F32)
            for r in range(1, 64):
                same = turn64(cells, r, line) == cells
                total = total + jnp.where(same, turn64(slots, r, line), 0.0)
            shared[pl.ds(at, 1), :] = total
            return jnp.where(number == (at.astype(F32)), 0.0, left)

        marked = jnp.max(flags, 1, keepdims=True) > 0.5
        left = jnp.where(jnp.broadcast_to(marked, (64, LANES)), number + 1.0, 0.0)
        lax.while_loop(lambda left: jnp.max(left) > 0.5, one_row, left)
        cur8[...] = cur8[...] + fetch(shared, rows, lanes)

    volts = fetch(ez_tab, rows, lanes) - fetch(curl_tab, rows, lanes) * cur8[...]
    next_ref[...] = volts
    current = across(apply(sum_ref, volts) + apply(damp_ref, volts_ref[...])) + base_ref[1:2, :]
    through = direct_ref[...] * own_ports(next_ref, index_x)
    current = current + jnp.where(index_y == 0, through, 0.0)
    owner = own_ref[...]
    low = owner & (LANES - 1)
    picked = jnp.where(
        ((owner >> 7) & 1) == 1, lookup(current[:, LANES:], low), lookup(current[:, :LANES], low)
    )
    picked = jnp.where((owner >> 8) == die * 4 + index_x, picked, 0.0)
    send_ref[pl.ds(0, 64, stride=2), :] = jnp.where(half, picked, 0.0)
    send_ref[pl.ds(1, 64, stride=2), :] = jnp.where(half, pltpu.roll(picked, 64, 1), 0.0)
    for k in range(states_ref.shape[1]):
        fade = decay_ref[0, k]
        for t in range(8):
            at = slice(t * LANES, (t + 1) * LANES)
            old = fade * state_ref[0, k : k + 1, at] + volts_ref[t : t + 1, :]
            states_ref[0, k : k + 1, at] = fade * old + volts[t : t + 1, :]


def source_kernel(
    e_in, recv_ref, owner_ref, line_ref, cell_ref, same_ref, mark_ref, e_ref, y_out, z_out, cur_tab, work
):
    del e_in
    for gx in range(4):
        for h in range(2):
            total = None
            for gy in range(4):
                part = recv_ref[pl.ds((gx * 4 + gy) * 32 + 1 + h, 8, stride=4), :]
                total = part if total is None else total + part
            cur_tab[pl.ds(gx * 2 + h, 8, stride=8), :] = total
    owner = jnp.concatenate([owner_ref[...], owner_ref[...]], 1)
    owner = jnp.broadcast_to(owner, (8, LANES))
    values = fetch(cur_tab, owner >> 7, owner & (LANES - 1))[0:1] * line_ref[0:1, :]
    add_sources(e_ref, (2,), cell_ref, values, same_ref, mark_ref, work)
    electric_edges(
        e_ref.shape[1],
        lambda c, i: e_ref[2 * c, i, 0:1, :],
        lambda c, i: e_ref[c, i, :, 0:LANES],
        y_out,
        z_out,
    )


def body(
    e_field, h_field, material, decay_table, curl_table, residues, pole_decay,
    pole_states, direct, port_cell, port_owner,
):
    field, (nx, ny, nz) = e_field.shape, material.shape
    slots = port_cell.shape[0]
    devices = lax.axis_size(ALL)
    rows, ports = residues.shape[2:]
    y_edge, z_edge = ((2 * nx, nz), F32), ((ny, LANES), F32)
    table = pltpu.VMEM((8, LANES), F32)
    cells = port_cell.reshape(1, slots)
    owners = port_owner.reshape(1, slots)

    def edges_back(y, z):
        return shifted(y, ("gx", "gy"), -1), shifted(z, "gz", -1)

    def edges_on(y, z):
        return shifted(y, ("gx", "gy"), 1), shifted(z, "gz", 1)

    pair = ((2,) + material.shape, F32)
    send, y, z = call(
        sample_kernel,
        (((devices, LANES), F32), y_edge, z_edge),
        (HBM, HBM, HBM),
        (
            pltpu.SMEM((slots,), I32),
            pltpu.VMEM((1, slots), I32),
            pltpu.VMEM((slots, 8, nz), F32),
            pltpu.VMEM((2, nx, 8, nz), F32),
            pltpu.VMEM((2, nx, ny, LANES), F32),
            pltpu.SemaphoreType.DMA((6,)),
        ),
    )(in_hbm(e_field), in_hbm(port_cell), in_hbm(owners))
    recv = lax.all_to_all(send, ALL, 0, 0, tiled=True)
    recv, y, z, fade, cells, curl_now = lax.optimization_barrier(
        (recv, y, z, pole_decay, cells, curl_table)
    )
    y, z = edges_back(y, z)
    magn, elec, e_held, h_held = call(
        factor_kernel,
        (pair, pair, (field, F32), (field, F32)),
        (HBM,) * 3 + (VMEM,) * 2 + (SMEM,),
        (
            table,
            pltpu.VMEM(material.shape, I32),
            pltpu.SemaphoreType.DMA((4,)),
            pltpu.SemaphoreType.DMA((2,)),
        ),
    )(in_hbm(material), in_hbm(e_field), in_hbm(h_field), decay_table, curl_table, curl_now)
    y, z, magn = lax.optimization_barrier((y, z, magn))
    h_one, y, z = call(h_kernel, ((field, F32), y_edge, z_edge), (VMEM,) * 5)(
        e_held, h_held, magn, y, z
    )
    y, z = edges_on(y, z)
    sums, damped, base = call(
        residue_kernel,
        (((rows, ports), F32), ((rows, ports), F32), ((8, rows), F32)),
        (VMEM, SMEM, VMEM),
        (pltpu.VMEM((8, ports), F32), pltpu.VMEM((2, rows, LANES), F32)),
    )(residues, fade, pole_states)
    line, same, mark = call(
        slot_kernel,
        (((8, LANES), F32), ((slots, slots), F32), ((slots, nz), F32)),
        (VMEM, VMEM, SMEM, VMEM),
        (table,),
    )(material, curl_table, port_cell, cells)
    own, at, volts, current = call(
        first_kernel,
        (((64, LANES), I32), ((2, 8, LANES), I32), ((8, LANES), F32), ((1, rows), F32)),
        (VMEM, VMEM, VMEM, VMEM),
        (pltpu.VMEM((64, LANES), F32),),
    )(recv, sums, base, direct)
    e_one, got = call(
        e_kernel, ((field, F32), ((1, LANES), F32)), (VMEM,) * 5 + (SMEM,)
    )(e_held, h_one, elec, y, z, port_cell)
    (send,) = call(pack_kernel, (((4 * devices, LANES), F32),), (VMEM,) * 3)(got, line, current)
    recv = lax.all_to_all(send, ALL, 0, 0, tiled=True)
    work = pltpu.VMEM((slots, nz), F32)
    e_one, y, z, currents = call(
        source_kernel,
        ((field, F32), y_edge, z_edge, ((64, LANES), F32)),
        (VMEM, VMEM, VMEM, VMEM, SMEM, VMEM, VMEM),
        (work,),
        aliases={0: 0},
    )(e_one, recv, owners, line, port_cell, same, mark)
    y, z = edges_back(y, z)
    states, send = call(
        second_kernel,
        ((pole_states.shape, F32), ((devices, LANES), F32)),
        (VMEM,) * 9 + (SMEM, VMEM),
        (
            pltpu.VMEM((64, LANES), F32),
            pltpu.VMEM((64, LANES), F32),
            pltpu.VMEM((64, LANES), F32),
            pltpu.VMEM((64, LANES), F32),
            pltpu.VMEM((8, LANES), F32),
            pltpu.VMEM((8, LANES), F32),
        ),
    )(recv, currents, own, at, volts, sums, damped, base, direct, pole_decay, pole_states)
    send, y, z = lax.optimization_barrier((send, y, z))
    h_two, y, z = call(h_kernel, ((field, F32), y_edge, z_edge), (VMEM,) * 5)(
        e_one, h_one, magn, y, z
    )
    y, z = edges_on(y, z)
    recv = lax.all_to_all(send, ALL, 0, 0, tiled=True)
    recv, y, z = lax.optimization_barrier((recv, y, z))
    e_out, h_out, ez = call(
        e_last_kernel,
        ((field, F32), (field, F32), (field[1:], F32)),
        (VMEM,) * 5,
        (
            pltpu.VMEM((2,) + field[1:], F32),
            pltpu.SemaphoreType.DMA((2,)),
            pltpu.SemaphoreType.DMA,
        ),
        specs_out=(HBM, HBM, VMEM),
    )(e_one, h_two, elec, y, z)
    e_out, _ = call(
        finish_kernel,
        ((field, F32), (field[1:], F32)),
        (HBM, VMEM, VMEM, VMEM, SMEM, VMEM, VMEM),
        (work, pltpu.SemaphoreType.DMA),
        aliases={0: 0, 1: 1},
        specs_out=(HBM, VMEM),
    )(e_out, ez, recv, line, port_cell, same, mark)
    return e_out, h_out, states


def solution(mesh):
    return jax.shard_map(
        body,
        mesh=mesh,
        in_specs=(
            P(None, None, ("gx", "gy"), "gz"),
            P(None, None, ("gx", "gy"), "gz"),
            P(None, ("gx", "gy"), "gz"),
            P(),
            P(),
            P("gz", "gy", "gx", None),
            P("gz", "gy"),
            P("gz", "gy", None),
            P("gz", "gx"),
            P(("gx", "gy", "gz")),
            P(("gx", "gy", "gz")),
        ),
        out_specs=(
            P(None, None, ("gx", "gy"), "gz"),
            P(None, None, ("gx", "gy"), "gz"),
            P("gz", "gy", None),
        ),
        check_vma=False,
    )
```

```python
import jax
import jax.numpy as jnp
from jax import lax
from jax.experimental import pallas as pl
from jax.experimental.pallas import tpu as pltpu
from jax.sharding import PartitionSpec as P


ALL = ("gx", "gy", "gz")
F32 = jnp.float32
I32 = jnp.int32
LANES = 128
UNROLL = 8
VMEM = pl.BlockSpec(memory_space=pltpu.VMEM)
SMEM = pl.BlockSpec(memory_space=pltpu.SMEM)
HBM = pl.BlockSpec(memory_space=pltpu.HBM)


def call(kernel, outs, ins, scratch=(), aliases=None, limit=16, specs_out=None):
    return pl.pallas_call(
        kernel,
        out_shape=tuple(jax.ShapeDtypeStruct(s, d) for s, d in outs),
        in_specs=list(ins),
        out_specs=tuple(specs_out) if specs_out else tuple(VMEM for _ in outs),
        scratch_shapes=list(scratch),
        input_output_aliases=aliases or {},
        compiler_params=pltpu.CompilerParams(vmem_limit_bytes=limit * 2**20),
    )


def in_hbm(value):
    return pltpu.with_memory_space_constraint(value, pltpu.HBM)


def shifted(value, axis, steps):
    count = lax.axis_size(axis)
    initial, last = (max(0, -steps), min(count, count - steps))
    return lax.ppermute(value, axis, [(source, source + steps) for source in range(initial, last)])


def lane_iota(shape):
    return lax.broadcasted_iota(I32, shape, len(shape) - 1)


def row_iota(shape):
    return lax.broadcasted_iota(I32, shape, 0)


def lookup(row, index):
    return jnp.take_along_axis(
        jnp.broadcast_to(row, index.shape), index, axis=1, mode="promise_in_bounds"
    )


def table_lookup(row, index):
    half = index.shape[1] // 2
    return jnp.concatenate([lookup(row, index[:, :half]), lookup(row, index[:, half:])], 1)


def tree_lookup(entries, bits):
    for bit in bits:
        entries = [
            jnp.where(bit, odd, even) for even, odd in zip(entries[0::2], entries[1::2])
        ]
    return entries[0]


def load_tables(scratch, decay_ref, curl_ref):
    scratch[...] = jnp.zeros_like(scratch)
    scratch[0:2, 0:16] = decay_ref[...]
    scratch[2:4, 0:16] = curl_ref[...]


def cell_of(cell):
    return cell >> 14, (cell >> 8) & 63, cell & 255


def sample_rows(read_row, cell_ref, count):
    lane = lane_iota((1, LANES))

    def step(slot, acc):
        i, y, k = cell_of(cell_ref[slot])
        row = read_row(i, y)
        half = jnp.where(k >= LANES, row[:, LANES:], row[:, :LANES])
        moved = pltpu.roll(half, (slot - k) & (LANES - 1), 1)
        return jnp.where(lane == slot, moved, acc)

    return lax.fori_loop(0, count, step, jnp.zeros((1, LANES), F32), unroll=count)


def split3(value):
    high = value.astype(jnp.bfloat16)
    rest = value - high.astype(F32)
    middle = rest.astype(jnp.bfloat16)
    return high, middle, (rest - middle.astype(F32)).astype(jnp.bfloat16)


def add_sources(field_ref, lead, cell_ref, values, same_ref, mark_ref, work):
    count = cell_ref.shape[0]
    scaled = same_ref[...] * values[:, :count]
    marks = mark_ref[...].astype(jnp.bfloat16)
    total = None
    for part in split3(scaled):
        product = jnp.dot(part, marks, preferred_element_type=F32)
        total = product if total is None else total + product
    work[...] = total
    for slot in range(count):
        i, y, _ = cell_of(cell_ref[slot])
        row = field_ref[lead + (i, pl.ds(y, 1))]
        work[slot : slot + 1, :] = row - work[slot : slot + 1, :]
    for slot in range(count):
        i, y, _ = cell_of(cell_ref[slot])
        field_ref[lead + (i, pl.ds(y, 1))] = work[slot : slot + 1, :]


def electric_edges(nx, first_row, first_tile, y_out, z_out):
    ny = z_out.shape[0]
    lane = lane_iota((ny, LANES))

    def step(i, acc):
        y_out[pl.ds(i, 1), :] = first_row(0, i)
        y_out[pl.ds(nx + i, 1), :] = first_row(1, i)
        for c in range(2):
            j = c * nx + i
            acc = jnp.where(lane == j, pltpu.roll(first_tile(c, i), j, 1), acc)
        return acc

    z_out[...] = lax.fori_loop(0, nx, step, jnp.zeros((ny, LANES), F32), unroll=6)


def factor_kernel(
    mat_ref, e_in, h_in, decay_ref, curl_ref, curl_sm,
    magn_ref, elec_ref, e_ref, h_ref, tab, sem,
):
    fields = [
        pltpu.make_async_copy(e_in, e_ref, sem.at[0]),
        pltpu.make_async_copy(h_in, h_ref, sem.at[1]),
    ]
    for copy in fields:
        copy.start()
    load_tables(tab, decay_ref, curl_ref)

    def step(i, carry):
        mat = mat_ref[i]
        bits = [(mat & (1 << b)) != 0 for b in range(4)]
        magn_ref[0, i] = table_lookup(tab[1:2, :], mat)
        magn_ref[1, i] = table_lookup(tab[3:4, :], mat)
        elec_ref[0, i] = table_lookup(tab[0:1, :], mat)
        elec_ref[1, i] = tree_lookup([curl_sm[0, n] for n in range(16)], bits)
        return carry

    lax.fori_loop(0, mat_ref.shape[0], step, 0, unroll=UNROLL)
    for copy in fields:
        copy.wait()


def h_kernel(e_ref, h_ref, magn_ref, yh_ref, zh_ref, out_ref, yl_ref, zl_ref):
    def factors(i):
        return magn_ref[0, i], magn_ref[1, i]

    acc = jnp.zeros(zl_ref.shape, F32)
    zl_ref[...] = h_update(
        factors, e_ref, h_ref, yh_ref, zh_ref, out_ref, yl_ref, acc, 0, e_ref.shape[1]
    )


def h_update(factors, e_ref, h_ref, yh_ref, zh_ref, out_ref, yl_ref, acc, begin, end):
    nx, ny, nz = e_ref.shape[1:]
    row = row_iota((ny, nz))
    lane = lane_iota((ny, LANES))

    def from_y(value, halo):
        return jnp.where(row == ny - 1, halo, pltpu.roll(value, ny - 1, 0))

    def from_z(value, j):
        moved = pltpu.roll(value, nz - 1, 1)
        halo = pltpu.roll(zh_ref[...], (LANES - 1 - j) & (LANES - 1), 1)
        right = jnp.where(lane == LANES - 1, halo, moved[:, nz - LANES :])
        return jnp.concatenate([moved[:, : nz - LANES], right], 1)

    def step(i, acc):
        decay, curl = factors(i)
        ex, ey, ez = e_ref[0, i], e_ref[1, i], e_ref[2, i]
        after = jnp.minimum(i + 1, nx - 1)
        inside = i < nx - 1
        ey_x = jnp.where(inside, e_ref[1, after], 0.0)
        ez_x = jnp.where(inside, e_ref[2, after], 0.0)
        hx = decay * h_ref[0, i] - curl * (
            (from_y(ez, yh_ref[pl.ds(nx + i, 1), :]) - ez) - (from_z(ey, nx + i) - ey)
        )
        hy = decay * h_ref[1, i] - curl * ((from_z(ex, i) - ex) - (ez_x - ez))
        hz = decay * h_ref[2, i] - curl * (
            (ey_x - ey) - (from_y(ex, yh_ref[pl.ds(i, 1), :]) - ex)
        )
        out_ref[0, i] = hx
        out_ref[1, i] = hy
        out_ref[2, i] = hz
        yl_ref[pl.ds(i, 1), :] = hx[ny - 1 : ny, :]
        yl_ref[pl.ds(nx + i, 1), :] = hz[ny - 1 : ny, :]
        for c, value in enumerate((hx, hy)):
            j = c * nx + i
            moved = pltpu.roll(value[:, nz - LANES :], (j + 1) & (LANES - 1), 1)
            acc = jnp.where(lane == j, moved, acc)
        return acc

    return lax.fori_loop(begin, end, step, acc, unroll=UNROLL)


def e_slab(i, e_ref, h_ref, elec_ref, yl_ref, zl_ref):
    nx, ny, nz = e_ref.shape[1:]
    row = row_iota((ny, nz))
    lane = lane_iota((ny, LANES))

    def from_y(value, halo):
        return jnp.where(row == 0, halo, pltpu.roll(value, 1, 0))

    def from_z(value, j):
        moved = pltpu.roll(value, 1, 1)
        halo = pltpu.roll(zl_ref[...], (LANES - j) & (LANES - 1), 1)
        left = jnp.where(lane == 0, halo, moved[:, :LANES])
        return jnp.concatenate([left, moved[:, LANES:]], 1)

    decay, curl = elec_ref[0, i], elec_ref[1, i]
    hx, hy, hz = h_ref[0, i], h_ref[1, i], h_ref[2, i]
    before = jnp.maximum(i - 1, 0)
    inside = i > 0
    hy_x = jnp.where(inside, h_ref[1, before], 0.0)
    hz_x = jnp.where(inside, h_ref[2, before], 0.0)
    ex = decay * e_ref[0, i] + curl * (
        (hz - from_y(hz, yl_ref[pl.ds(nx + i, 1), :])) - (hy - from_z(hy, nx + i))
    )
    ey = decay * e_ref[1, i] + curl * ((hx - from_z(hx, i)) - (hz - hz_x))
    ez = decay * e_ref[2, i] + curl * (
        (hy - hy_x) - (hx - from_y(hx, yl_ref[pl.ds(i, 1), :]))
    )
    return ex, ey, ez


def e_kernel(e_ref, h_ref, elec_ref, yl_ref, zl_ref, cell_ref, out_ref, got_ref, y_out, z_out):
    def step(i, carry):
        ex, ey, ez = e_slab(i, e_ref, h_ref, elec_ref, yl_ref, zl_ref)
        out_ref[0, i] = ex
        out_ref[1, i] = ey
        out_ref[2, i] = ez
        return carry

    lax.fori_loop(0, e_ref.shape[1], step, 0, unroll=UNROLL)
    got_ref[...] = sample_rows(
        lambda i, y: out_ref[2, i, pl.ds(y, 1), :], cell_ref, cell_ref.shape[0]
    )
    electric_edges(
        out_ref.shape[1],
        lambda c, i: out_ref[2 * c, i, 0:1, :],
        lambda c, i: out_ref[c, i, :, 0:LANES],
        y_out,
        z_out,
    )


def e_last_kernel(
    e_ref, h_ref, elec_ref, yl_ref, zl_ref, got_ref, line_ref, cell_ref, same_ref, mark_ref,
    e_out, h_out, buf, work, sem, h_sem,
):
    nx = e_ref.shape[1]
    h_copy = pltpu.make_async_copy(h_ref, h_out, h_sem)
    h_copy.start()

    def step(i, carry):
        ex, ey, ez = e_slab(i, e_ref, h_ref, elec_ref, yl_ref, zl_ref)
        buf[0, i] = ex
        buf[1, i] = ey
        buf[2, i] = ez
        for c in range(2):
            pltpu.make_async_copy(buf.at[c, i], e_out.at[c, i], sem.at[c]).start()
        return carry

    lax.fori_loop(0, nx, step, 0, unroll=UNROLL)
    values = jnp.sum(got_ref[...], 0, keepdims=True) * line_ref[0:1, :]
    add_sources(buf, (2,), cell_ref, values, same_ref, mark_ref, work)
    last = pltpu.make_async_copy(buf.at[2], e_out.at[2], sem.at[2])
    last.start()
    for c in range(2):
        pltpu.make_async_copy(buf.at[c], e_out.at[c], sem.at[c]).wait()
    h_copy.wait()
    last.wait()


def sample_kernel(
    e_ref, cell_in, owner_in, mat_in, send_ref, y_out, z_out, mat_out,
    cell_ref, owner_ref, slabs, rows, tiles, sems,
):
    count, nx = cell_in.shape[0], e_ref.shape[1]
    cell_copy = pltpu.make_async_copy(cell_in, cell_ref, sems.at[0])
    cell_copy.start()
    owner_copy = pltpu.make_async_copy(owner_in, owner_ref, sems.at[1])
    owner_copy.start()
    y_copies = [
        pltpu.make_async_copy(e_ref.at[2 * c, :, 0:8], rows.at[c], sems.at[4 + c])
        for c in range(2)
    ]
    for copy in y_copies:
        copy.start()
    z_copy = pltpu.make_async_copy(e_ref.at[0:2, :, :, 0:LANES], tiles, sems.at[3])
    z_copy.start()
    cell_copy.wait()
    for slot in range(count):
        i, y, _ = cell_of(cell_ref[slot])
        block = pl.ds(pl.multiple_of((y >> 3) << 3, 8), 8)
        pltpu.make_async_copy(e_ref.at[2, i, block], slabs.at[slot], sems.at[2]).start()
    mat_copy = pltpu.make_async_copy(mat_in, mat_out, sems.at[6])
    mat_copy.start()
    for copy in y_copies:
        copy.wait()
    z_copy.wait()
    electric_edges(
        nx, lambda c, i: rows[c, i, 0:1, :], lambda c, i: tiles[c, i], y_out, z_out
    )
    owner_copy.wait()
    pltpu.make_async_copy(slabs, slabs, sems.at[2]).wait()
    lane = lane_iota((1, LANES))
    got = jnp.zeros((1, LANES), F32)
    for slot in range(count):
        _, y, k = cell_of(cell_ref[slot])
        row = slabs[slot, pl.ds(y & 7, 1), :]
        half = jnp.where(k >= LANES, row[:, LANES:], row[:, :LANES])
        got = jnp.where(lane == slot, pltpu.roll(half, (slot - k) & (LANES - 1), 1), got)
    owner = owner_ref[...].astype(F32)
    line = jnp.concatenate([got[:, :count], owner], 1)
    send_ref[...] = jnp.broadcast_to(line, send_ref.shape)
    mat_copy.wait()


def slot_kernel(mat_ref, curl_ref, cell_ref, cells_ref, line_ref, same_ref, mark_ref, tab):
    count = cell_ref.shape[0]
    tab[...] = jnp.zeros_like(tab)
    tab[0:1, 0:16] = curl_ref[0:1, :]
    kinds = sample_rows(
        lambda i, y: mat_ref[i, pl.ds(y, 1), :].astype(F32), cell_ref, count
    )
    curl = lookup(tab[0:1, :], jnp.broadcast_to(kinds, (8, LANES)).astype(I32))[0:1]
    cells = cells_ref[...]
    cells = jnp.concatenate([cells, cells], 1)
    twin = jnp.zeros((1, LANES), F32)
    for r in range(1, count):
        twin = jnp.where(pltpu.roll(cells, r, 1) == cells, 1.0, twin)
    lane = lane_iota((1, LANES))
    line_ref[0:1, :] = jnp.where(lane < count, curl, 0.0)
    wide = lane_iota((1, mark_ref.shape[1]))
    grid_row = cells_ref[...] >> 8
    for slot in range(count):
        cell = cell_ref[slot]
        same_ref[slot : slot + 1, :] = jnp.where(grid_row == (cell >> 8), 1.0, 0.0)
        mark_ref[slot : slot + 1, :] = jnp.where(wide == (cell & 255), 1.0, 0.0)
    line_ref[1:2, :] = jnp.where(lane < count, cells.astype(F32), twin)


def across(value):
    return jnp.concatenate(
        [jnp.sum(value[h : h + LANES].T, 0, keepdims=True) for h in (0, LANES)], 1
    )


def residue_kernel(res_ref, decay_ref, state_ref, sum_ref, damp_ref, base_ref, line, acc):
    poles, rows, ports = res_ref.shape[1:]
    tiles = ports // LANES
    for k in range(poles):
        line[k : k + 1, :] = decay_ref[0, k] * state_ref[0, k : k + 1, :]
        line[poles + k : poles + k + 1, :] = decay_ref[0, k] * line[k : k + 1, :]

    def step(block, carry):
        at = pl.ds(pl.multiple_of(block * 8, 8), 8)
        one = jnp.zeros((8, LANES), F32)
        two = jnp.zeros((8, LANES), F32)
        for t in range(tiles):
            lanes = slice(t * LANES, (t + 1) * LANES)
            total = damp = None
            for k in range(poles):
                value = res_ref[0, k, at, lanes]
                one = one + value * line[k : k + 1, lanes]
                two = two + value * line[poles + k : poles + k + 1, lanes]
                scaled = decay_ref[0, k] * value
                total = value if total is None else total + value
                damp = scaled if damp is None else damp + scaled
            sum_ref[at, lanes] = total
            damp_ref[at, lanes] = damp
        acc[0, at, :] = one
        acc[1, at, :] = two
        return carry

    lax.fori_loop(0, rows // 8, step, 0, unroll=UNROLL)
    base_ref[0:1, :] = across(acc[0])
    base_ref[1:2, :] = across(acc[1])


def apply(mat_ref, volts):
    total = None
    for t in range(volts.shape[0]):
        part = mat_ref[:, t * LANES : (t + 1) * LANES] * volts[t : t + 1, :]
        total = part if total is None else total + part
    return total


def fetch(tab_ref, rows, lanes):
    acc = jnp.zeros(lanes.shape, F32)
    for r in range(tab_ref.shape[0]):
        acc = jnp.where(rows == r, lookup(tab_ref[r : r + 1, :], lanes), acc)
    return acc


def own_ports(volts_ref, index_x):
    return jnp.concatenate(
        [volts_ref[pl.ds(2 * index_x + h, 1), :] for h in range(2)], 1
    )


def first_kernel(recv_ref, sum_ref, base_ref, direct_ref, own_ref, at_ref, volts_ref, cur_ref, tab):
    index_x, index_y, die = (lax.axis_index(name) for name in ALL)
    half = lane_iota((64, LANES)) < 64
    even = recv_ref[pl.ds(0, 64, stride=2), :]
    odd = recv_ref[pl.ds(1, 64, stride=2), :]
    tab[...] = jnp.where(half, even, pltpu.roll(odd, 64, 1))
    owner = jnp.where(half, pltpu.roll(even, 64, 1), odd).astype(I32)
    own_ref[...] = owner
    high, low = owner >> 7, owner & (LANES - 1)
    port = die * 8 + row_iota((8, LANES))
    lane = lane_iota((8, LANES)).astype(F32)
    spot = row_iota((LANES, LANES))
    found = jnp.zeros((16, LANES), F32)
    for r in range(0, 64, 2):
        picks, marks = [], []
        for q in (r, r + 1):
            mine = high[q : q + 1, :] == port
            picks.append(
                jnp.concatenate(
                    [jnp.where(mine, float(q), 0.0), jnp.where(mine, lane, 0.0)], 0
                ).astype(jnp.bfloat16)
            )
            marks.append(
                jnp.where(low[q : q + 1, :] == spot, 1.0, 0.0).astype(jnp.bfloat16)
            )
        found = found + lax.dot_general(
            jnp.concatenate(picks, 1),
            jnp.concatenate(marks, 1),
            (((1,), (1,)), ((), ())),
            preferred_element_type=F32,
        )
    found = found.astype(I32)
    rows, lanes = found[0:8], found[8:16]
    at_ref[0] = rows
    at_ref[1] = lanes
    volts = fetch(tab, rows, lanes)
    volts_ref[...] = volts
    current = across(apply(sum_ref, volts)) + base_ref[0:1, :]
    through = direct_ref[...] * own_ports(volts_ref, index_x)
    cur_ref[...] = current + jnp.where(index_y == 0, through, 0.0)


def pack_kernel(got_ref, line_ref, cur_ref, send_ref):
    lane = lane_iota((1, LANES))
    first = jnp.where(lane < 64, got_ref[...], pltpu.roll(line_ref[0:1, :], 64, 1))
    shape = (8, LANES)
    turn = row_iota(shape) & 3
    block = jnp.where(turn == 0, first, jnp.where(turn == 3, line_ref[1:2, :], 0.0))
    block = jnp.where(turn == 1, cur_ref[:, :LANES], block)
    block = jnp.where(turn == 2, cur_ref[:, LANES:], block)

    def step(n, carry):
        send_ref[pl.ds(pl.multiple_of(n * 8, 8), 8), :] = block
        return carry

    lax.fori_loop(0, send_ref.shape[0] // 8, step, 0, unroll=8)


def turn64(value, r, lane):
    return jnp.where(
        (lane & 63) >= r, pltpu.roll(value, r, 1), pltpu.roll(value, (r + 64) & (LANES - 1), 1)
    )


def second_kernel(
    recv_ref, cur_tab, own_ref, at_ref, volts_ref, sum_ref, damp_ref, base_ref, direct_ref,
    decay_ref, state_ref,
    states_ref, send_ref,
    ez_tab, curl_tab, cell_tab, shared, cur8, next_ref,
):
    index_x, index_y, die = (lax.axis_index(name) for name in ALL)
    half = lane_iota((64, LANES)) < 64
    even = recv_ref[pl.ds(0, 64, stride=8), :]
    odd = recv_ref[pl.ds(4, 64, stride=8), :]
    ez_tab[...] = jnp.where(half, even, pltpu.roll(odd, 64, 1))
    curl_tab[...] = jnp.where(half, pltpu.roll(even, 64, 1), odd)
    rows, lanes = at_ref[0], at_ref[1]
    cur8[...] = cur_tab[pl.ds(pl.multiple_of(die * 8, 8), 8), :]

    even = recv_ref[pl.ds(3, 64, stride=8), :]
    odd = recv_ref[pl.ds(7, 64, stride=8), :]
    flags = jnp.where(half, 0.0, jnp.maximum(even, odd))

    @pl.when(jnp.max(flags) > 0.5)
    def _():
        cell_tab[...] = jnp.where(half, even, pltpu.roll(odd, 64, 1))
        shared[...] = jnp.zeros_like(shared)
        number = row_iota((64, LANES)).astype(F32)
        line = lane_iota((1, LANES))

        def one_row(left):
            at = jnp.max(left).astype(I32) - 1
            cells = cell_tab[pl.ds(at, 1), :]
            owner = jnp.broadcast_to(own_ref[pl.ds(at, 1), :], (8, LANES))
            slots = fetch(cur_tab, owner >> 7, owner & (LANES - 1))[0:1]
            total = jnp.zeros((1, LANES), F32)
            for r in range(1, 64):
                same = turn64(cells, r, line) == cells
                total = total + jnp.where(same, turn64(slots, r, line), 0.0)
            shared[pl.ds(at, 1), :] = total
            return jnp.where(number == (at.astype(F32)), 0.0, left)

        marked = jnp.max(flags, 1, keepdims=True) > 0.5
        left = jnp.where(jnp.broadcast_to(marked, (64, LANES)), number + 1.0, 0.0)
        lax.while_loop(lambda left: jnp.max(left) > 0.5, one_row, left)
        cur8[...] = cur8[...] + fetch(shared, rows, lanes)

    volts = fetch(ez_tab, rows, lanes) - fetch(curl_tab, rows, lanes) * cur8[...]
    next_ref[...] = volts
    current = across(apply(sum_ref, volts) + apply(damp_ref, volts_ref[...])) + base_ref[1:2, :]
    through = direct_ref[...] * own_ports(next_ref, index_x)
    current = current + jnp.where(index_y == 0, through, 0.0)
    owner = own_ref[...]
    low = owner & (LANES - 1)
    picked = jnp.where(
        ((owner >> 7) & 1) == 1, lookup(current[:, LANES:], low), lookup(current[:, :LANES], low)
    )
    picked = jnp.where((owner >> 8) == die * 4 + index_x, picked, 0.0)
    send_ref[pl.ds(0, 64, stride=2), :] = jnp.where(half, picked, 0.0)
    send_ref[pl.ds(1, 64, stride=2), :] = jnp.where(half, pltpu.roll(picked, 64, 1), 0.0)
    for k in range(states_ref.shape[1]):
        fade = decay_ref[0, k]
        for t in range(8):
            at = slice(t * LANES, (t + 1) * LANES)
            old = fade * state_ref[0, k : k + 1, at] + volts_ref[t : t + 1, :]
            states_ref[0, k : k + 1, at] = fade * old + volts[t : t + 1, :]


def next_block_sources(recv_ref, own_ref, cur_tab, y_in, y_out):
    index_x, index_y, die = (lax.axis_index(name) for name in ALL)
    block = index_x * 4 + index_y + 1
    exists = block < 16
    device = jnp.where(exists, block * 8 + die, 0)
    curl = pltpu.roll(recv_ref[pl.ds(4 * device, 1), :], 64, 1)
    cells = recv_ref[pl.ds(4 * device + 3, 1), :].astype(I32)
    owner = own_ref[pl.ds(device >> 1, 1), :]
    owner = jnp.where((device & 1) == 1, pltpu.roll(owner, 64, 1), owner)
    owner = jnp.broadcast_to(owner, (8, LANES))
    values = fetch(cur_tab, owner >> 7, owner & (LANES - 1))[0:1] * curl
    i, y, k = cell_of(cells)
    lane = lane_iota((1, LANES))
    values = jnp.where((lane < 64) & (y == 0), jnp.where(exists, values, 0.0), 0.0)
    planes, lanes = y_in.shape
    line = row_iota((planes, LANES)) - planes // 2
    spread = jnp.where(line == i, values, 0.0)
    marks = jnp.where(row_iota((lanes, LANES)) == k, 1.0, 0.0).astype(jnp.bfloat16)
    total = y_in[...]
    for part in split3(spread):
        total = total - lax.dot_general(
            part, marks, (((1,), (1,)), ((), ())), preferred_element_type=F32
        )
    y_out[...] = total


def source_kernel(
    e_in, recv_ref, owner_ref, own_ref, line_ref, cell_ref, same_ref, mark_ref, y_in,
    e_ref, y_out, cur_tab, work,
):
    del e_in
    for gx in range(4):
        for h in range(2):
            total = None
            for gy in range(4):
                part = recv_ref[pl.ds((gx * 4 + gy) * 32 + 1 + h, 8, stride=4), :]
                total = part if total is None else total + part
            cur_tab[pl.ds(gx * 2 + h, 8, stride=8), :] = total
    owner = jnp.concatenate([owner_ref[...], owner_ref[...]], 1)
    owner = jnp.broadcast_to(owner, (8, LANES))
    values = fetch(cur_tab, owner >> 7, owner & (LANES - 1))[0:1] * line_ref[0:1, :]
    add_sources(e_ref, (2,), cell_ref, values, same_ref, mark_ref, work)
    next_block_sources(recv_ref, own_ref, cur_tab, y_in, y_out)


def body(
    e_field, h_field, material, decay_table, curl_table, residues, pole_decay,
    pole_states, direct, port_cell, port_owner,
):
    field, (nx, ny, nz) = e_field.shape, material.shape
    slots = port_cell.shape[0]
    devices = lax.axis_size(ALL)
    rows, ports = residues.shape[2:]
    y_edge, z_edge = ((2 * nx, nz), F32), ((ny, LANES), F32)
    table = pltpu.VMEM((8, LANES), F32)
    cells = port_cell.reshape(1, slots)
    owners = port_owner.reshape(1, slots)

    def edges_back(y, z):
        return shifted(y, ("gx", "gy"), -1), shifted(z, "gz", -1)

    def edges_on(y, z):
        return shifted(y, ("gx", "gy"), 1), shifted(z, "gz", 1)

    pair = ((2,) + material.shape, F32)
    send, y, z, kinds = call(
        sample_kernel,
        (((devices, LANES), F32), y_edge, z_edge, (material.shape, I32)),
        (HBM,) * 4,
        (
            pltpu.SMEM((slots,), I32),
            pltpu.VMEM((1, slots), I32),
            pltpu.VMEM((slots, 8, nz), F32),
            pltpu.VMEM((2, nx, 8, nz), F32),
            pltpu.VMEM((2, nx, ny, LANES), F32),
            pltpu.SemaphoreType.DMA((7,)),
        ),
    )(in_hbm(e_field), in_hbm(port_cell), in_hbm(owners), in_hbm(material))
    y, z = edges_back(y, z)
    recv = lax.all_to_all(send, ALL, 0, 0, tiled=True)
    recv, y, z, fade, cells, curl_now = lax.optimization_barrier(
        (recv, y, z, pole_decay, cells, curl_table)
    )
    magn, elec, e_held, h_held = call(
        factor_kernel,
        (pair, pair, (field, F32), (field, F32)),
        (VMEM, HBM, HBM) + (VMEM,) * 2 + (SMEM,),
        (table, pltpu.SemaphoreType.DMA((2,))),
    )(kinds, in_hbm(e_field), in_hbm(h_field), decay_table, curl_table, curl_now)
    y, z, magn = lax.optimization_barrier((y, z, magn))
    h_one, y, z = call(h_kernel, ((field, F32), y_edge, z_edge), (VMEM,) * 5)(
        e_held, h_held, magn, y, z
    )
    y, z = edges_on(y, z)
    sums, damped, base = call(
        residue_kernel,
        (((rows, ports), F32), ((rows, ports), F32), ((8, rows), F32)),
        (VMEM, SMEM, VMEM),
        (pltpu.VMEM((8, ports), F32), pltpu.VMEM((2, rows, LANES), F32)),
    )(residues, fade, pole_states)
    line, same, mark = call(
        slot_kernel,
        (((8, LANES), F32), ((slots, slots), F32), ((slots, nz), F32)),
        (VMEM, VMEM, SMEM, VMEM),
        (table,),
    )(kinds, curl_table, port_cell, cells)
    own, at, volts, current = call(
        first_kernel,
        (((64, LANES), I32), ((2, 8, LANES), I32), ((8, LANES), F32), ((1, rows), F32)),
        (VMEM, VMEM, VMEM, VMEM),
        (pltpu.VMEM((64, LANES), F32),),
    )(recv, sums, base, direct)
    e_one, got, y, z = call(
        e_kernel, ((field, F32), ((1, LANES), F32), y_edge, z_edge), (VMEM,) * 5 + (SMEM,)
    )(e_held, h_one, elec, y, z, port_cell)
    (send,) = call(pack_kernel, (((4 * devices, LANES), F32),), (VMEM,) * 3)(got, line, current)
    y, z = edges_back(y, z)
    recv = lax.all_to_all(send, ALL, 0, 0, tiled=True)
    recv, y, z = lax.optimization_barrier((recv, y, z))
    work = pltpu.VMEM((slots, nz), F32)
    e_one, y, currents = call(
        source_kernel,
        ((field, F32), y_edge, ((64, LANES), F32)),
        (VMEM,) * 5 + (SMEM,) + (VMEM,) * 3,
        (work,),
        aliases={0: 0},
    )(e_one, recv, owners, own, line, port_cell, same, mark, y)
    states, send = call(
        second_kernel,
        ((pole_states.shape, F32), ((devices, LANES), F32)),
        (VMEM,) * 9 + (SMEM, VMEM),
        (
            pltpu.VMEM((64, LANES), F32),
            pltpu.VMEM((64, LANES), F32),
            pltpu.VMEM((64, LANES), F32),
            pltpu.VMEM((64, LANES), F32),
            pltpu.VMEM((8, LANES), F32),
            pltpu.VMEM((8, LANES), F32),
        ),
    )(recv, currents, own, at, volts, sums, damped, base, direct, pole_decay, pole_states)
    send, y, z = lax.optimization_barrier((send, y, z))
    h_two, y, z = call(h_kernel, ((field, F32), y_edge, z_edge), (VMEM,) * 5)(
        e_one, h_one, magn, y, z
    )
    y, z = edges_on(y, z)
    recv = lax.all_to_all(send, ALL, 0, 0, tiled=True)
    recv, y, z = lax.optimization_barrier((recv, y, z))
    e_out, h_out = call(
        e_last_kernel,
        ((field, F32), (field, F32)),
        (VMEM,) * 7 + (SMEM, VMEM, VMEM),
        (
            pltpu.VMEM(field, F32),
            work,
            pltpu.SemaphoreType.DMA((3,)),
            pltpu.SemaphoreType.DMA,
        ),
        specs_out=(HBM, HBM),
    )(e_one, h_two, elec, y, z, recv, line, port_cell, same, mark)
    return e_out, h_out, states


def solution(mesh):
    return jax.shard_map(
        body,
        mesh=mesh,
        in_specs=(
            P(None, None, ("gx", "gy"), "gz"),
            P(None, None, ("gx", "gy"), "gz"),
            P(None, ("gx", "gy"), "gz"),
            P(),
            P(),
            P("gz", "gy", "gx", None),
            P("gz", "gy"),
            P("gz", "gy", None),
            P("gz", "gx"),
            P(("gx", "gy", "gz")),
            P(("gx", "gy", "gz")),
        ),
        out_specs=(
            P(None, None, ("gx", "gy"), "gz"),
            P(None, None, ("gx", "gy"), "gz"),
            P("gz", "gy", None),
        ),
        check_vma=False,
    )
```
